32 devices in a mesh: energy: 8 (over y, x, core), space: 4 (over z).
Axes of the slice: x: 2, y: 2, z: 4, core: 2. Of those that a mesh axis runs over, the one named last changes fastest.
Arguments:
- green0: float32 [16, 8, 2, 128, 128], P('energy', 'space'), may hold values from -6 to 6
- grad_h: float32 [8, 8, 128, 128], P('space'), may hold values from -0.5 to 0.5
- neighbours: int32 [8, 8], P('space'), may hold values from 0 to 7, as said below
- shifts: int32 [4], replicated, may hold values from -2 to 2, as said below
- coupling: float32 [4], replicated, may hold values from 0.0002 to 0.0006
Outputs:
- green: float32 [16, 8, 2, 128, 128], P('energy', 'space')
The draws below stay inside these ranges and needn't reach their ends.
Inputs may be any that keep to these rules, and one draw needn't show every extreme that they name: |neighbours[a, k] - a| <= 2; entry 0 of atom a is max(a - 2, 0) and entry 1 is min(a + 2, 7). The values 2 and -2 each stand at some position of shifts.
All inputs are finite; a program needn't handle non-finite values.
Results may differ from the reference program's by a relative error of at most 0.0001.
Values sent between devices are 32-bit elements; how exact they have to be, the bound alone decides.
No kernel may reach another device: no remote copies, remote signals or barrier semaphores. Data moves between devices by JAX's collectives and lax.ppermute only.
A program may use at most 64 MiB of HBM per device.

```python
import math
import jax
import jax.numpy as jnp
from jax import lax

ORB = 128
NB = 8
SHIFTS = 4
REACH = 2
ITERS = 2
NE = 16
ATOMS = 8


def draw_neighbours(key, part):
    offsets = jax.random.randint(jax.random.fold_in(key, 11), (ATOMS, NB), -REACH, REACH + 1)
    offsets = offsets.at[:, 0].set(-REACH).at[:, 1].set(REACH)
    atoms = jnp.arange(ATOMS, dtype=jnp.int32)[:, None]
    return jnp.clip(atoms + offsets, 0, ATOMS - 1).astype(jnp.int32)


def draw_shifts(key, part):
    others = jax.random.randint(jax.random.fold_in(key, 23), (SHIFTS - 2,), -REACH, REACH + 1).astype(jnp.int32)
    values = jnp.concatenate([jnp.array([REACH, -REACH], dtype=jnp.int32), others])
    order = jax.random.permutation(jax.random.fold_in(key, 29), SHIFTS)
    return values[order].astype(jnp.int32)


def level_of(stream_key, shape, split, least, top_value):
    loudness = 1.0
    for axis_at, shards_of in split:
        draws = jax.random.uniform(jax.random.fold_in(jax.random.fold_in(stream_key, 6), axis_at), (shards_of,), jnp.float32, least / len(split), top_value / len(split))
        loudness = loudness * jnp.repeat(jnp.exp(draws), shape[axis_at] // shards_of).reshape((-1,) + (1,) * (len(shape) - 1 - axis_at))
    return loudness


def gaussian(key, shape, scale, bound, split=(), kind=jnp.bfloat16):
    entries = jax.random.normal(key, shape, jnp.float32) * scale
    if len(split) > 0:
        entries = level_of(key, shape, split, -0.22, 0.18) * entries
    return jnp.clip(entries, min=-bound, max=bound).astype(kind)


def setup_inputs(seed: int = 0) -> dict:
    key_of = jax.random.split(jax.random.key(seed), 6)
    return {
        "green0": gaussian(key_of[0], (NE, ATOMS, 2, ORB, ORB), 1.0, 6.0, ((0, 8), (1, 4)), jnp.float32),
        "grad_h": gaussian(key_of[1], (ATOMS, NB, ORB, ORB), ORB ** -0.5, 0.5, ((0, 4),), jnp.float32),
        "neighbours": draw_neighbours(jax.random.fold_in(key_of[5], 71), 0),
        "shifts": draw_shifts(jax.random.fold_in(key_of[5], 71), 0),
        "coupling": jnp.clip(jnp.exp(jax.random.uniform(key_of[4], (SHIFTS,), jnp.float32, math.log(0.0002), math.log(0.0006))), 0.0002, 0.0006),
    }


def complex_mul(left, right):
    hp = lax.Precision.HIGHEST
    lre, lim = left[:, 0], left[:, 1]
    rre, rim = right[:, 0], right[:, 1]
    real = jnp.einsum('aij,ajk->aik', lre, rre, precision=hp) - jnp.einsum('aij,ajk->aik', lim, rim, precision=hp)
    imag = jnp.einsum('aij,ajk->aik', lre, rim, precision=hp) + jnp.einsum('aij,ajk->aik', lim, rre, precision=hp)
    return jnp.stack([real, imag], axis=1)


def reference(green0, grad_h, neighbours, shifts, coupling):
    hp = lax.Precision.HIGHEST
    green = green0
    for step in range(ITERS):
        padded = jnp.pad(green, ((REACH, REACH), (0, 0), (0, 0), (0, 0), (0, 0)))
        summed = jnp.zeros_like(green)
        for shift_index in range(SHIFTS):
            start = (REACH + shifts[shift_index]).astype(jnp.int32)
            summed = summed + coupling[shift_index] * lax.dynamic_slice_in_dim(padded, start, NE, 0)

        def one_energy(pair):
            summed_e, base_e = pair
            picked = summed_e[neighbours]
            left = jnp.einsum('akij,akcjl->akcil', grad_h, picked, precision=hp)
            sigma = jnp.einsum('akcil,akml->acim', left, grad_h, precision=hp)
            return base_e + complex_mul(complex_mul(base_e, sigma), base_e)

        green = lax.map(one_energy, (summed, green0))
    return green
```

```python
import functools

import jax
import jax.numpy as jnp
from jax import lax
from jax.experimental import pallas as pl
from jax.experimental.pallas import tpu as pltpu
from jax.sharding import PartitionSpec as P

REACH = 2
ITERS = 2
VMEM = pl.BlockSpec(memory_space=pltpu.VMEM)
SMEM = pl.BlockSpec(memory_space=pltpu.SMEM)


def swaps(count, parity):
    pairs, i = [(j, j) for j in range(parity)], parity
    while i + 1 < count:
        pairs += [(i, i + 1), (i + 1, i)]
        i += 2
    if i < count:
        pairs.append((i, i))
    return pairs


def partners(axis):
    even = lax.axis_index(axis) % 2 == 0
    first = jnp.where(even, 1, -1)
    return first, -first


def trade(cells, axis, dim):
    count, own = lax.axis_size(axis), cells.shape[dim]
    got = []
    for parity, side in enumerate(partners(axis)):
        edge = cells
        if own != REACH:
            edge = lax.dynamic_slice_in_dim(cells, jnp.where(side > 0, own - REACH, 0), REACH, dim)
        got.append(lax.ppermute(edge, axis, swaps(count, parity)))
    return got


def split(value):
    high = value.astype(jnp.bfloat16)
    return high, (value - high.astype(jnp.float32)).astype(jnp.bfloat16)


def dot(left, right):
    return lax.dot_general(left, right, (((1,), (0,)), ((), ())), preferred_element_type=jnp.float32)


def prepare_kernel(grad_ref, right_ref, left_ref):
    atoms, entries, orb, _ = grad_ref.shape
    for a in range(atoms):
        for k in range(entries):
            high, low = split(grad_ref[a, k])
            left_ref[a, :orb, k * orb : (k + 1) * orb] = high
            left_ref[a, orb:, k * orb : (k + 1) * orb] = low
            high, low = split(grad_ref[a, k].T)
            right_ref[a, k, :, :orb] = high
            right_ref[a, k, :, orb:] = low


def prepare(grad_h):
    atoms, entries, orb, _ = grad_h.shape
    return pl.pallas_call(
        prepare_kernel,
        out_shape=(
            jax.ShapeDtypeStruct((atoms, entries, orb, 2 * orb), jnp.bfloat16),
            jax.ShapeDtypeStruct((atoms, 2 * orb, entries * orb), jnp.bfloat16),
        ),
        in_specs=[VMEM],
        out_specs=(VMEM, VMEM),
        name="prepare",
    )(grad_h)


def sandwich_kernel(index_ref, right_ref, left_ref, own_ref, one_ref, two_ref, out_ref, green_ref, high_ref, low_ref):
    energies, atoms, parts, orb, _ = out_ref.shape
    entries = right_ref.shape[1]
    at = 0
    for ref in (own_ref, one_ref, two_ref):
        for a in range(ref.shape[1]):
            for e in range(energies):
                for c in range(parts):
                    row = (e * parts + c) * orb
                    high, low = split(ref[e, a, c])
                    green_ref[at, row : row + orb, :orb] = high
                    green_ref[at, row : row + orb, orb:] = low
            at += 1
    for a in range(atoms):
        for k in range(entries):
            weight = right_ref[a, k]
            both = dot(green_ref[index_ref[a, k]], jnp.concatenate([weight, weight], axis=0))
            high, low = split(both[:, :orb] + both[:, orb:])
            for b in range(energies * parts):
                here = (slice(k * orb, (k + 1) * orb), slice(b * orb, (b + 1) * orb))
                high_ref[here] = high[b * orb : (b + 1) * orb]
                low_ref[here] = low[b * orb : (b + 1) * orb]
        main = dot(left_ref[a], high_ref[...])
        total = main[:orb] + (main[orb:] + dot(left_ref[a, :orb], low_ref[...]))
        for e in range(energies):
            for c in range(parts):
                col = (e * parts + c) * orb
                out_ref[e, a, c] = total[:, col : col + orb]


def sandwich(index, right, left, own, one, two):
    energies, atoms, parts, orb, _ = own.shape
    entries = right.shape[1]
    sources = atoms + one.shape[1] + two.shape[1]
    wide = energies * parts * orb
    return pl.pallas_call(
        sandwich_kernel,
        out_shape=jax.ShapeDtypeStruct(own.shape, jnp.float32),
        in_specs=[SMEM] + [VMEM] * 5,
        out_specs=VMEM,
        scratch_shapes=[
            pltpu.VMEM((sources, wide, 2 * orb), jnp.bfloat16),
            pltpu.VMEM((entries * orb, wide), jnp.bfloat16),
            pltpu.VMEM((entries * orb, wide), jnp.bfloat16),
        ],
        name="sandwich",
    )(index, right, left, own, one, two)


def complex_product(left, right):
    high, low = split(jnp.concatenate(left, axis=1))
    block = jnp.concatenate([jnp.concatenate(right, axis=1), jnp.concatenate([-right[1], right[0]], axis=1)], axis=0)
    block_high, block_low = split(block)
    orb = left[0].shape[0]
    main = dot(jnp.concatenate([high, low], axis=0), block_high)
    total = main[:orb] + (main[orb:] + dot(high, block_low))
    return total[:, :orb], total[:, orb:]


def dyson_kernel(weight_ref, own_ref, one_ref, two_ref, base_ref, out_ref):
    energies, atoms, parts, orb, _ = out_ref.shape
    sources = [(ref, s) for ref in (own_ref, one_ref, two_ref) for s in range(ref.shape[0])]
    for e in range(energies):
        for a in range(atoms):
            sigma = []
            for c in range(parts):
                total = jnp.zeros((orb, orb), jnp.float32)
                for at, (ref, s) in enumerate(sources):
                    total = total + weight_ref[e, at] * ref[s, a, c]
                sigma.append(total)
            base = (base_ref[e, a, 0], base_ref[e, a, 1])
            real, imag = complex_product(complex_product(base, sigma), base)
            out_ref[e, a, 0] = base[0] + real
            out_ref[e, a, 1] = base[1] + imag


def dyson(weights, own, one, two, base):
    return pl.pallas_call(
        dyson_kernel,
        out_shape=jax.ShapeDtypeStruct(base.shape, jnp.float32),
        in_specs=[SMEM] + [VMEM] * 4,
        out_specs=VMEM,
        name="dyson",
    )(weights, own, one, two, base)


def source_index(neighbours, atoms):
    away = neighbours - lax.axis_index("space") * atoms
    first, _ = partners("space")
    below = jnp.where(first < 0, atoms, atoms + REACH) + away + REACH
    above = jnp.where(first > 0, atoms, atoms + REACH) + away - atoms
    return jnp.where(away < 0, below, jnp.where(away < atoms, away, above)).astype(jnp.int32)


def shift_weights(shifts, coupling, energies):
    here, last = lax.axis_index("energy"), lax.axis_size("energy") - 1
    columns = [(jnp.arange(energies), True)]
    for side in partners("energy"):
        start = jnp.where(side > 0, energies, -REACH)
        there = here + side
        columns.append((start + jnp.arange(REACH), (there >= 0) & (there <= last)))
    source = jnp.concatenate([c for c, _ in columns])
    valid = jnp.concatenate([jnp.broadcast_to(jnp.asarray(v), c.shape) for c, v in columns])
    distance = source[None, :] - jnp.arange(energies)[:, None]
    hit = (distance[:, :, None] == shifts) & valid[None, :, None]
    return jnp.sum(jnp.where(hit, coupling, 0.0), axis=-1)


def per_device(green0, grad_h, neighbours, shifts, coupling):
    energies, atoms = green0.shape[:2]
    right, left = prepare(grad_h)
    index = source_index(neighbours, atoms)
    weights = shift_weights(shifts, coupling, energies)
    green = green0
    for step in range(ITERS):
        inner = sandwich(index, right, left, green, *trade(green, "space", 1))
        green = dyson(weights, inner, *trade(inner, "energy", 0), green0)
    return green


def solution(mesh):
    return jax.shard_map(
        per_device,
        mesh=mesh,
        in_specs=(
            P("energy", "space", None, None, None),
            P("space", None, None, None),
            P("space", None),
            P(),
            P(),
        ),
        out_specs=P("energy", "space", None, None, None),
        check_vma=False,
    )
```

```python
import functools

import jax
import jax.numpy as jnp
from jax import lax
from jax.experimental import pallas as pl
from jax.experimental.pallas import tpu as pltpu
from jax.sharding import PartitionSpec as P

AXES = ("energy", "space")
REACH = 2
ITERS = 2
VMEM = pl.BlockSpec(memory_space=pltpu.VMEM)
SMEM = pl.BlockSpec(memory_space=pltpu.SMEM)


def near(*arrays):
    return [pltpu.with_memory_space_constraint(a, pltpu.VMEM) for a in arrays]


def at_hand(shape, dtype=jnp.float32):
    return pltpu.VMEM(shape, dtype)


def swaps(axis, parity):
    sizes = {name: lax.axis_size(name) for name in AXES}
    count, pairs = sizes[axis], []
    for energy in range(sizes["energy"]):
        for space in range(sizes["space"]):
            to = {"energy": energy, "space": space}
            there = to[axis] + (1 if to[axis] % 2 == parity else -1)
            if 0 <= there < count:
                to[axis] = there
            elif axis == "space" and sizes["energy"] % 2 == 0:
                to["energy"] = energy ^ 1
            elif axis == "energy" and count % 2 == 0:
                to["energy"] = there % count
            pairs.append((energy * sizes["space"] + space, to["energy"] * sizes["space"] + to["space"]))
    return pairs


def partners(axis):
    even = lax.axis_index(axis) % 2 == 0
    first = jnp.where(even, 1, -1)
    return first, -first


def trade(cells, axis, dim):
    own = cells.shape[dim]
    got = []
    for parity, side in enumerate(partners(axis)):
        edge = cells
        if own != REACH:
            edge = lax.dynamic_slice_in_dim(cells, jnp.where(side > 0, own - REACH, 0), REACH, dim)
        got.append(lax.ppermute(edge, AXES, swaps(axis, parity)))
    return got


def split(value):
    high = value.astype(jnp.bfloat16)
    return high, (value - high.astype(jnp.float32)).astype(jnp.bfloat16)


def dot(left, right):
    return lax.dot_general(left, right, (((1,), (0,)), ((), ())), preferred_element_type=jnp.float32)


def prepare_kernel(grad_ref, right_ref, left_ref):
    atoms, entries, orb, _ = grad_ref.shape
    for a in range(atoms):
        for k in range(entries):
            high, low = split(grad_ref[a, k])
            left_ref[a, :orb, k * orb : (k + 1) * orb] = high
            left_ref[a, orb:, k * orb : (k + 1) * orb] = low
            high, low = split(grad_ref[a, k].T)
            right_ref[a, k, :, :orb] = high
            right_ref[a, k, :, orb:] = low


def prepare(grad_h):
    atoms, entries, orb, _ = grad_h.shape
    return pl.pallas_call(
        prepare_kernel,
        out_shape=(
            at_hand((atoms, entries, orb, 2 * orb), jnp.bfloat16),
            at_hand((atoms, 2 * orb, entries * orb), jnp.bfloat16),
        ),
        in_specs=[VMEM],
        out_specs=(VMEM, VMEM),
        compiler_params=pltpu.CompilerParams(vmem_limit_bytes=24 << 20),
        name="prepare",
    )(grad_h)


def sandwich_kernel(index_ref, right_ref, left_ref, own_ref, one_ref, two_ref, out_ref, green_ref, high_ref, low_ref):
    energies, atoms, parts, orb, _ = out_ref.shape
    entries = right_ref.shape[1]
    at = 0
    for ref in (own_ref, one_ref, two_ref):
        for a in range(ref.shape[1]):
            for e in range(energies):
                for c in range(parts):
                    row = (e * parts + c) * orb
                    high, low = split(ref[e, a, c])
                    green_ref[at, row : row + orb, :orb] = high
                    green_ref[at, row : row + orb, orb:] = low
            at += 1
    for a in range(atoms):
        for k in range(entries):
            weight = right_ref[a, k]
            both = dot(green_ref[index_ref[a, k]], jnp.concatenate([weight, weight], axis=0))
            high, low = split(both[:, :orb] + both[:, orb:])
            for b in range(energies * parts):
                here = (slice(k * orb, (k + 1) * orb), slice(b * orb, (b + 1) * orb))
                high_ref[here] = high[b * orb : (b + 1) * orb]
                low_ref[here] = low[b * orb : (b + 1) * orb]
        main = dot(left_ref[a], high_ref[...])
        total = main[:orb] + (main[orb:] + dot(left_ref[a, :orb], low_ref[...]))
        for e in range(energies):
            for c in range(parts):
                col = (e * parts + c) * orb
                out_ref[e, a, c] = total[:, col : col + orb]


def sandwich(index, right, left, own, one, two):
    energies, atoms, parts, orb, _ = own.shape
    entries = right.shape[1]
    sources = atoms + one.shape[1] + two.shape[1]
    wide = energies * parts * orb
    return pl.pallas_call(
        sandwich_kernel,
        out_shape=at_hand(own.shape),
        in_specs=[SMEM] + [VMEM] * 5,
        out_specs=VMEM,
        scratch_shapes=[
            pltpu.VMEM((sources, wide, 2 * orb), jnp.bfloat16),
            pltpu.VMEM((entries * orb, wide), jnp.bfloat16),
            pltpu.VMEM((entries * orb, wide), jnp.bfloat16),
        ],
        compiler_params=pltpu.CompilerParams(vmem_limit_bytes=24 << 20),
        name="sandwich",
    )(index, *near(right, left, own, one, two))


def complex_product(left, right):
    high, low = split(jnp.concatenate(left, axis=1))
    block = jnp.concatenate([jnp.concatenate(right, axis=1), jnp.concatenate([-right[1], right[0]], axis=1)], axis=0)
    block_high, block_low = split(block)
    orb = left[0].shape[0]
    main = dot(jnp.concatenate([high, low], axis=0), block_high)
    total = main[:orb] + (main[orb:] + dot(high, block_low))
    return total[:, :orb], total[:, orb:]


def dyson_kernel(weight_ref, own_ref, one_ref, two_ref, base_ref, out_ref):
    energies, atoms, parts, orb, _ = out_ref.shape
    sources = [(ref, s) for ref in (own_ref, one_ref, two_ref) for s in range(ref.shape[0])]
    for e in range(energies):
        for a in range(atoms):
            sigma = []
            for c in range(parts):
                total = jnp.zeros((orb, orb), jnp.float32)
                for at, (ref, s) in enumerate(sources):
                    total = total + weight_ref[e, at] * ref[s, a, c]
                sigma.append(total)
            base = (base_ref[e, a, 0], base_ref[e, a, 1])
            real, imag = complex_product(complex_product(base, sigma), base)
            out_ref[e, a, 0] = base[0] + real
            out_ref[e, a, 1] = base[1] + imag


def dyson(weights, own, one, two, base):
    return pl.pallas_call(
        dyson_kernel,
        out_shape=jax.ShapeDtypeStruct(base.shape, jnp.float32),
        in_specs=[SMEM] + [VMEM] * 4,
        out_specs=VMEM,
        compiler_params=pltpu.CompilerParams(vmem_limit_bytes=24 << 20),
        name="dyson",
    )(weights, *near(own, one, two, base))


def source_index(neighbours, atoms):
    away = neighbours - lax.axis_index("space") * atoms
    first, _ = partners("space")
    below = jnp.where(first < 0, atoms, atoms + REACH) + away + REACH
    above = jnp.where(first > 0, atoms, atoms + REACH) + away - atoms
    return jnp.where(away < 0, below, jnp.where(away < atoms, away, above)).astype(jnp.int32)


def shift_weights(shifts, coupling, energies):
    here, last = lax.axis_index("energy"), lax.axis_size("energy") - 1
    columns = [(jnp.arange(energies), True)]
    for side in partners("energy"):
        start = jnp.where(side > 0, energies, -REACH)
        there = here + side
        columns.append((start + jnp.arange(REACH), (there >= 0) & (there <= last)))
    source = jnp.concatenate([c for c, _ in columns])
    valid = jnp.concatenate([jnp.broadcast_to(jnp.asarray(v), c.shape) for c, v in columns])
    distance = source[None, :] - jnp.arange(energies)[:, None]
    hit = (distance[:, :, None] == shifts) & valid[None, :, None]
    return jnp.sum(jnp.where(hit, coupling, 0.0), axis=-1)


def per_device(green0, grad_h, neighbours, shifts, coupling):
    energies, atoms = green0.shape[:2]
    right, left = prepare(grad_h)
    index = source_index(neighbours, atoms)
    weights = shift_weights(shifts, coupling, energies)
    green = green0
    for step in range(ITERS):
        inner = sandwich(index, right, left, green, *trade(green, "space", 1))
        green = dyson(weights, inner, *trade(inner, "energy", 0), green0)
    return green


def solution(mesh):
    return jax.shard_map(
        per_device,
        mesh=mesh,
        in_specs=(
            P("energy", "space", None, None, None),
            P("space", None, None, None),
            P("space", None),
            P(),
            P(),
        ),
        out_specs=P("energy", "space", None, None, None),
        check_vma=False,
    )
```

```python
import jax
import jax.numpy as jnp
from jax import lax
from jax.experimental import pallas as pl
from jax.experimental.pallas import tpu as pltpu
from jax.sharding import PartitionSpec as P

AXES = ("energy", "space")
REACH = 2
ITERS = 2
VMEM = pl.BlockSpec(memory_space=pltpu.VMEM)
SMEM = pl.BlockSpec(memory_space=pltpu.SMEM)
PARAMS = pltpu.CompilerParams(vmem_limit_bytes=24 << 20)


def near(*arrays):
    return [pltpu.with_memory_space_constraint(a, pltpu.VMEM) for a in arrays]


def at_hand(shape, dtype=jnp.float32):
    return pltpu.VMEM(shape, dtype)


def swaps(axis, parity):
    sizes = {name: lax.axis_size(name) for name in AXES}
    count, pairs = sizes[axis], []
    for energy in range(sizes["energy"]):
        for space in range(sizes["space"]):
            to = {"energy": energy, "space": space}
            there = to[axis] + (1 if to[axis] % 2 == parity else -1)
            if 0 <= there < count:
                to[axis] = there
            elif axis == "space" and sizes["energy"] % 2 == 0:
                to["energy"] = energy ^ 1
            elif axis == "energy" and count % 2 == 0:
                to["energy"] = there % count
            pairs.append((energy * sizes["space"] + space, to["energy"] * sizes["space"] + to["space"]))
    return pairs


def partners(axis):
    even = lax.axis_index(axis) % 2 == 0
    first = jnp.where(even, 1, -1)
    return first, -first


def trade(cells, axis, dim):
    own = cells.shape[dim]
    got = []
    for parity, side in enumerate(partners(axis)):
        edge = cells
        if own != REACH:
            edge = lax.dynamic_slice_in_dim(cells, jnp.where(side > 0, own - REACH, 0), REACH, dim)
        got.append(lax.ppermute(edge, AXES, swaps(axis, parity)))
    return got


def split(value):
    high = value.astype(jnp.bfloat16)
    return high, (value - high.astype(jnp.float32)).astype(jnp.bfloat16)


def dot(left, right):
    return lax.dot_general(left, right, (((1,), (0,)), ((), ())), preferred_element_type=jnp.float32)


def prepare_kernel(grad_ref, right_ref, left_ref):
    atoms, entries, orb, _ = grad_ref.shape
    for a in range(atoms):
        for k in range(entries):
            high, low = split(grad_ref[a, k])
            left_ref[a, :orb, k * orb : (k + 1) * orb] = high
            left_ref[a, orb:, k * orb : (k + 1) * orb] = low
            high, low = split(grad_ref[a, k].T)
            right_ref[a, k, :, :orb] = high
            right_ref[a, k, :, orb:] = low


def prepare(grad_h):
    atoms, entries, orb, _ = grad_h.shape
    return pl.pallas_call(
        prepare_kernel,
        out_shape=(
            at_hand((atoms, entries, orb, 2 * orb), jnp.bfloat16),
            at_hand((atoms, 2 * orb, entries * orb), jnp.bfloat16),
        ),
        in_specs=[VMEM],
        out_specs=(VMEM, VMEM),
        compiler_params=PARAMS,
        name="prepare",
    )(grad_h)


def sandwich_kernel(index_ref, right_ref, left_ref, own_ref, one_ref, two_ref, out_ref, green_ref, high_ref, low_ref):
    energies, atoms, orb, _ = out_ref.shape
    entries = right_ref.shape[1]
    at = 0
    for ref in (own_ref, one_ref, two_ref):
        for a in range(ref.shape[1]):
            for e in range(energies):
                high, low = split(ref[e, a])
                green_ref[at, e * orb : (e + 1) * orb, :orb] = high
                green_ref[at, e * orb : (e + 1) * orb, orb:] = low
            at += 1
    for a in range(atoms):
        for k in range(entries):
            weight = right_ref[a, k]
            both = dot(green_ref[index_ref[a, k]], jnp.concatenate([weight, weight], axis=0))
            high, low = split(both[:, :orb] + both[:, orb:])
            for e in range(energies):
                here = (slice(k * orb, (k + 1) * orb), slice(e * orb, (e + 1) * orb))
                high_ref[here] = high[e * orb : (e + 1) * orb]
                low_ref[here] = low[e * orb : (e + 1) * orb]
        main = dot(left_ref[a], high_ref[...])
        total = main[:orb] + (main[orb:] + dot(left_ref[a, :orb], low_ref[...]))
        for e in range(energies):
            out_ref[e, a] = total[:, e * orb : (e + 1) * orb]


def sandwich(index, right, left, own, one, two):
    energies, atoms, orb, _ = own.shape
    entries = right.shape[1]
    sources = atoms + one.shape[1] + two.shape[1]
    return pl.pallas_call(
        sandwich_kernel,
        out_shape=at_hand(own.shape),
        in_specs=[SMEM] + [VMEM] * 5,
        out_specs=VMEM,
        scratch_shapes=[
            pltpu.VMEM((sources, energies * orb, 2 * orb), jnp.bfloat16),
            pltpu.VMEM((entries * orb, energies * orb), jnp.bfloat16),
            pltpu.VMEM((entries * orb, energies * orb), jnp.bfloat16),
        ],
        compiler_params=PARAMS,
        name="sandwich",
    )(index, *near(right, left, own, one, two))


def parts_kernel(green_ref, real_ref, imag_ref, sems):
    copies = [pltpu.make_async_copy(green_ref.at[:, :, c], ref, sems.at[c]) for c, ref in enumerate((real_ref, imag_ref))]
    for copy in copies:
        copy.start()
    for copy in copies:
        copy.wait()


def parts(green):
    shape = green.shape[:2] + green.shape[3:]
    return pl.pallas_call(
        parts_kernel,
        out_shape=(at_hand(shape), at_hand(shape)),
        in_specs=[pl.BlockSpec(memory_space=pltpu.HBM)],
        out_specs=(VMEM, VMEM),
        scratch_shapes=[pltpu.SemaphoreType.DMA((2,))],
        compiler_params=PARAMS,
        name="parts",
    )(green)


def shifted(weight_ref, refs, e, a):
    sources = [(ref, s) for ref in refs for s in range(ref.shape[0])]
    total = weight_ref[e, 0] * sources[0][0][sources[0][1], a]
    for at, (ref, s) in enumerate(sources[1:]):
        total = total + weight_ref[e, at + 1] * ref[s, a]
    return total


def shift_sum_kernel(weight_ref, own_ref, one_ref, two_ref, out_ref):
    for e in range(out_ref.shape[0]):
        for a in range(out_ref.shape[1]):
            out_ref[e, a] = shifted(weight_ref, (own_ref, one_ref, two_ref), e, a)


def shift_sum(weights, own, one, two):
    return pl.pallas_call(
        shift_sum_kernel,
        out_shape=at_hand(own.shape),
        in_specs=[SMEM] + [VMEM] * 3,
        out_specs=VMEM,
        compiler_params=PARAMS,
        name="shift_sum",
    )(weights, *near(own, one, two))


def complex_product(left, right):
    high, low = split(jnp.concatenate(left, axis=1))
    block = jnp.concatenate([jnp.concatenate(right, axis=1), jnp.concatenate([-right[1], right[0]], axis=1)], axis=0)
    block_high, block_low = split(block)
    orb = left[0].shape[0]
    main = dot(jnp.concatenate([high, low], axis=0), block_high)
    total = main[:orb] + (main[orb:] + dot(high, block_low))
    return total[:, :orb], total[:, orb:]


def dyson_kernel(weight_ref, sigma_ref, own_ref, one_ref, two_ref, real_ref, imag_ref, *out_refs):
    for e in range(real_ref.shape[0]):
        for a in range(real_ref.shape[1]):
            sigma = (sigma_ref[e, a], shifted(weight_ref, (own_ref, one_ref, two_ref), e, a))
            base = (real_ref[e, a], imag_ref[e, a])
            moved = complex_product(complex_product(base, sigma), base)
            for c in range(2):
                if len(out_refs) == 2:
                    out_refs[c][e, a] = base[c] + moved[c]
                else:
                    out_refs[0][e, a, c] = base[c] + moved[c]


def dyson(weights, sigma, own, one, two, base, whole):
    shape = base[0].shape
    if whole:
        out_shape = jax.ShapeDtypeStruct(shape[:2] + (2,) + shape[2:], jnp.float32)
    else:
        out_shape = (at_hand(shape), at_hand(shape))
    return pl.pallas_call(
        dyson_kernel,
        out_shape=out_shape,
        in_specs=[SMEM] + [VMEM] * 6,
        out_specs=VMEM if whole else (VMEM, VMEM),
        compiler_params=PARAMS,
        name="dyson",
    )(weights, *near(sigma, own, one, two, *base))


def source_index(neighbours, atoms):
    away = neighbours - lax.axis_index("space") * atoms
    first, _ = partners("space")
    below = jnp.where(first < 0, atoms, atoms + REACH) + away + REACH
    above = jnp.where(first > 0, atoms, atoms + REACH) + away - atoms
    return jnp.where(away < 0, below, jnp.where(away < atoms, away, above)).astype(jnp.int32)


def shift_weights(shifts, coupling, energies):
    here, last = lax.axis_index("energy"), lax.axis_size("energy") - 1
    columns = [(jnp.arange(energies), True)]
    for side in partners("energy"):
        start = jnp.where(side > 0, energies, -REACH)
        there = here + side
        columns.append((start + jnp.arange(REACH), (there >= 0) & (there <= last)))
    source = jnp.concatenate([c for c, _ in columns])
    valid = jnp.concatenate([jnp.broadcast_to(jnp.asarray(v), c.shape) for c, v in columns])
    distance = source[None, :] - jnp.arange(energies)[:, None]
    hit = (distance[:, :, None] == shifts) & valid[None, :, None]
    return jnp.sum(jnp.where(hit, coupling, 0.0), axis=-1)


def per_device(green0, grad_h, neighbours, shifts, coupling):
    energies, atoms = green0.shape[:2]
    base = real, imag = parts(green0)
    right, left = prepare(grad_h)
    index = source_index(neighbours, atoms)
    weights = shift_weights(shifts, coupling, energies)
    for step in range(ITERS):
        real_beside = trade(real, "energy", 0)
        imag_beside = trade(imag, "space", 1)
        summed = shift_sum(weights, real, *real_beside)
        summed_beside = trade(summed, "space", 1)
        inner = sandwich(index, right, left, imag, *imag_beside)
        inner_beside = trade(inner, "energy", 0)
        sigma = sandwich(index, right, left, summed, *summed_beside)
        green = dyson(weights, sigma, inner, *inner_beside, base, step == ITERS - 1)
        if step < ITERS - 1:
            real, imag = green
    return green


def solution(mesh):
    return jax.shard_map(
        per_device,
        mesh=mesh,
        in_specs=(
            P("energy", "space", None, None, None),
            P("space", None, None, None),
            P("space", None),
            P(),
            P(),
        ),
        out_specs=P("energy", "space", None, None, None),
        check_vma=False,
    )
```

```python
import jax
import jax.numpy as jnp
from jax import lax
from jax.experimental import pallas as pl
from jax.experimental.pallas import tpu as pltpu
from jax.sharding import PartitionSpec as P

AXES = ("energy", "space")
REACH = 2
ITERS = 2
VMEM = pl.BlockSpec(memory_space=pltpu.VMEM)
SMEM = pl.BlockSpec(memory_space=pltpu.SMEM)
PARAMS = pltpu.CompilerParams(vmem_limit_bytes=24 << 20)


def near(*arrays):
    return [pltpu.with_memory_space_constraint(a, pltpu.VMEM) for a in arrays]


def at_hand(shape, dtype=jnp.float32):
    return pltpu.VMEM(shape, dtype)


def swaps(axis, parity):
    sizes = {name: lax.axis_size(name) for name in AXES}
    count, pairs = sizes[axis], []
    for energy in range(sizes["energy"]):
        for space in range(sizes["space"]):
            to = {"energy": energy, "space": space}
            there = to[axis] + (1 if to[axis] % 2 == parity else -1)
            if 0 <= there < count:
                to[axis] = there
            elif axis == "space" and sizes["energy"] % 2 == 0:
                to["energy"] = energy ^ 1
            elif axis == "energy" and count % 2 == 0:
                to["space"] = space ^ 1
            pairs.append((energy * sizes["space"] + space, to["energy"] * sizes["space"] + to["space"]))
    return pairs


def partners(axis):
    even = lax.axis_index(axis) % 2 == 0
    first = jnp.where(even, 1, -1)
    return first, -first


def trade(cells, axis, dim):
    own = cells.shape[dim]
    got = []
    for parity, side in enumerate(partners(axis)):
        edge = cells
        if own != REACH:
            edge = lax.dynamic_slice_in_dim(cells, jnp.where(side > 0, own - REACH, 0), REACH, dim)
        got.append(lax.ppermute(edge, AXES, swaps(axis, parity)))
    return got


def split(value):
    high = value.astype(jnp.bfloat16)
    return high, (value - high.astype(jnp.float32)).astype(jnp.bfloat16)


def dot(left, right):
    return lax.dot_general(left, right, (((1,), (0,)), ((), ())), preferred_element_type=jnp.float32)


def prepare_kernel(grad_ref, right_ref, left_ref):
    atoms, entries, orb, _ = grad_ref.shape
    for a in range(atoms):
        for k in range(entries):
            high, low = split(grad_ref[a, k])
            left_ref[a, :orb, k * orb : (k + 1) * orb] = high
            left_ref[a, orb:, k * orb : (k + 1) * orb] = low
            high, low = split(grad_ref[a, k].T)
            right_ref[a, k, :, :orb] = high
            right_ref[a, k, :, orb:] = low


def prepare(grad_h):
    atoms, entries, orb, _ = grad_h.shape
    return pl.pallas_call(
        prepare_kernel,
        out_shape=(
            at_hand((atoms, entries, orb, 2 * orb), jnp.bfloat16),
            at_hand((atoms, 2 * orb, entries * orb), jnp.bfloat16),
        ),
        in_specs=[VMEM],
        out_specs=(VMEM, VMEM),
        compiler_params=PARAMS,
        name="prepare",
    )(grad_h)


def sandwich_kernel(index_ref, right_ref, left_ref, own_ref, one_ref, two_ref, out_ref, green_ref, high_ref, low_ref):
    energies, atoms, orb, _ = out_ref.shape
    entries = right_ref.shape[1]
    at = 0
    for ref in (own_ref, one_ref, two_ref):
        for a in range(ref.shape[1]):
            for e in range(energies):
                high, low = split(ref[e, a])
                green_ref[at, e * orb : (e + 1) * orb, :orb] = high
                green_ref[at, e * orb : (e + 1) * orb, orb:] = low
            at += 1
    for a in range(atoms):
        for k in range(entries):
            weight = right_ref[a, k]
            both = dot(green_ref[index_ref[a, k]], jnp.concatenate([weight, weight], axis=0))
            high, low = split(both[:, :orb] + both[:, orb:])
            for e in range(energies):
                here = (slice(k * orb, (k + 1) * orb), slice(e * orb, (e + 1) * orb))
                high_ref[here] = high[e * orb : (e + 1) * orb]
                low_ref[here] = low[e * orb : (e + 1) * orb]
        main = dot(left_ref[a], high_ref[...])
        total = main[:orb] + (main[orb:] + dot(left_ref[a, :orb], low_ref[...]))
        for e in range(energies):
            out_ref[e, a] = total[:, e * orb : (e + 1) * orb]


def sandwich(index, right, left, own, one, two):
    energies, atoms, orb, _ = own.shape
    entries = right.shape[1]
    sources = atoms + one.shape[1] + two.shape[1]
    return pl.pallas_call(
        sandwich_kernel,
        out_shape=at_hand(own.shape),
        in_specs=[SMEM] + [VMEM] * 5,
        out_specs=VMEM,
        scratch_shapes=[
            pltpu.VMEM((sources, energies * orb, 2 * orb), jnp.bfloat16),
            pltpu.VMEM((entries * orb, energies * orb), jnp.bfloat16),
            pltpu.VMEM((entries * orb, energies * orb), jnp.bfloat16),
        ],
        compiler_params=PARAMS,
        name="sandwich",
    )(index, *near(right, left, own, one, two))


def parts_kernel(green_ref, real_ref, imag_ref, sems):
    copies = [pltpu.make_async_copy(green_ref.at[:, :, c], ref, sems.at[c]) for c, ref in enumerate((real_ref, imag_ref))]
    for copy in copies:
        copy.start()
    for copy in copies:
        copy.wait()


def parts(green):
    shape = green.shape[:2] + green.shape[3:]
    return pl.pallas_call(
        parts_kernel,
        out_shape=(at_hand(shape), at_hand(shape)),
        in_specs=[pl.BlockSpec(memory_space=pltpu.HBM)],
        out_specs=(VMEM, VMEM),
        scratch_shapes=[pltpu.SemaphoreType.DMA((2,))],
        compiler_params=PARAMS,
        name="parts",
    )(pltpu.with_memory_space_constraint(green, pltpu.HBM))


def shifted(weight_ref, refs, e, a):
    sources = [(ref, s) for ref in refs for s in range(ref.shape[0])]
    total = weight_ref[e, 0] * sources[0][0][sources[0][1], a]
    for at, (ref, s) in enumerate(sources[1:]):
        total = total + weight_ref[e, at + 1] * ref[s, a]
    return total


def shift_sum_kernel(weight_ref, own_ref, one_ref, two_ref, out_ref):
    for e in range(out_ref.shape[0]):
        for a in range(out_ref.shape[1]):
            out_ref[e, a] = shifted(weight_ref, (own_ref, one_ref, two_ref), e, a)


def shift_sum(weights, own, one, two):
    return pl.pallas_call(
        shift_sum_kernel,
        out_shape=at_hand(own.shape),
        in_specs=[SMEM] + [VMEM] * 3,
        out_specs=VMEM,
        compiler_params=PARAMS,
        name="shift_sum",
    )(weights, *near(own, one, two))


def complex_product(left, right):
    high, low = split(jnp.concatenate(left, axis=1))
    block = jnp.concatenate([jnp.concatenate(right, axis=1), jnp.concatenate([-right[1], right[0]], axis=1)], axis=0)
    block_high, block_low = split(block)
    orb = left[0].shape[0]
    main = dot(jnp.concatenate([high, low], axis=0), block_high)
    total = main[:orb] + (main[orb:] + dot(high, block_low))
    return total[:, :orb], total[:, orb:]


def dyson_kernel(weight_ref, sigma_ref, own_ref, one_ref, two_ref, real_ref, imag_ref, *out_refs):
    for e in range(real_ref.shape[0]):
        for a in range(real_ref.shape[1]):
            sigma = (sigma_ref[e, a], shifted(weight_ref, (own_ref, one_ref, two_ref), e, a))
            base = (real_ref[e, a], imag_ref[e, a])
            moved = complex_product(complex_product(base, sigma), base)
            for c in range(2):
                if len(out_refs) == 2:
                    out_refs[c][e, a] = base[c] + moved[c]
                else:
                    out_refs[0][e, a, c] = base[c] + moved[c]


def dyson(weights, sigma, own, one, two, base, whole):
    shape = base[0].shape
    if whole:
        out_shape = jax.ShapeDtypeStruct(shape[:2] + (2,) + shape[2:], jnp.float32)
    else:
        out_shape = (at_hand(shape), at_hand(shape))
    return pl.pallas_call(
        dyson_kernel,
        out_shape=out_shape,
        in_specs=[SMEM] + [VMEM] * 6,
        out_specs=VMEM if whole else (VMEM, VMEM),
        compiler_params=PARAMS,
        name="dyson",
    )(weights, *near(sigma, own, one, two, *base))


def source_index(neighbours, atoms):
    away = neighbours - lax.axis_index("space") * atoms
    first, _ = partners("space")
    below = jnp.where(first < 0, atoms, atoms + REACH) + away + REACH
    above = jnp.where(first > 0, atoms, atoms + REACH) + away - atoms
    return jnp.where(away < 0, below, jnp.where(away < atoms, away, above)).astype(jnp.int32)


def shift_weights(shifts, coupling, energies):
    here, last = lax.axis_index("energy"), lax.axis_size("energy") - 1
    columns = [(jnp.arange(energies), True)]
    for side in partners("energy"):
        start = jnp.where(side > 0, energies, -REACH)
        there = here + side
        columns.append((start + jnp.arange(REACH), (there >= 0) & (there <= last)))
    source = jnp.concatenate([c for c, _ in columns])
    valid = jnp.concatenate([jnp.broadcast_to(jnp.asarray(v), c.shape) for c, v in columns])
    distance = source[None, :] - jnp.arange(energies)[:, None]
    hit = (distance[:, :, None] == shifts) & valid[None, :, None]
    return jnp.sum(jnp.where(hit, coupling, 0.0), axis=-1)


def per_device(green0, grad_h, neighbours, shifts, coupling):
    energies, atoms = green0.shape[:2]
    base = real, imag = parts(green0)
    right, left = prepare(grad_h)
    index = source_index(neighbours, atoms)
    weights = shift_weights(shifts, coupling, energies)
    for step in range(ITERS):
        real_beside = trade(real, "energy", 0)
        imag_beside = trade(imag, "space", 1)
        summed = shift_sum(weights, real, *real_beside)
        summed_beside = trade(summed, "space", 1)
        inner = sandwich(index, right, left, imag, *imag_beside)
        inner_beside = trade(inner, "energy", 0)
        sigma = sandwich(index, right, left, summed, *summed_beside)
        green = dyson(weights, sigma, inner, *inner_beside, base, step == ITERS - 1)
        if step < ITERS - 1:
            real, imag = green
    return green


def solution(mesh):
    return jax.shard_map(
        per_device,
        mesh=mesh,
        in_specs=(
            P("energy", "space", None, None, None),
            P("space", None, None, None),
            P("space", None),
            P(),
            P(),
        ),
        out_specs=P("energy", "space", None, None, None),
        check_vma=False,
    )
```

```python
import jax
import jax.numpy as jnp
from jax import lax
from jax.experimental import pallas as pl
from jax.experimental.pallas import tpu as pltpu
from jax.sharding import PartitionSpec as P

AXES = ("energy", "space")
REACH = 2
ITERS = 2
VMEM = pl.BlockSpec(memory_space=pltpu.VMEM)
SMEM = pl.BlockSpec(memory_space=pltpu.SMEM)
PARAMS = pltpu.CompilerParams(vmem_limit_bytes=24 << 20)


def near(*arrays):
    return [pltpu.with_memory_space_constraint(a, pltpu.VMEM) for a in arrays]


def at_hand(shape, dtype=jnp.float32):
    return pltpu.VMEM(shape, dtype)


def swaps(axis, parity):
    sizes = {name: lax.axis_size(name) for name in AXES}
    count, pairs = sizes[axis], []
    for energy in range(sizes["energy"]):
        for space in range(sizes["space"]):
            to = {"energy": energy, "space": space}
            there = to[axis] + (1 if to[axis] % 2 == parity else -1)
            if 0 <= there < count:
                to[axis] = there
            elif axis == "space" and sizes["energy"] % 2 == 0:
                to["energy"] = energy ^ 1
            elif axis == "energy" and count % 2 == 0:
                to["space"] = space ^ 1
            pairs.append((energy * sizes["space"] + space, to["energy"] * sizes["space"] + to["space"]))
    return pairs


def partners(axis):
    even = lax.axis_index(axis) % 2 == 0
    first = jnp.where(even, 1, -1)
    return first, -first


def trade(cells, axis, dim):
    own = cells.shape[dim]
    got = []
    for parity, side in enumerate(partners(axis)):
        edge = cells
        if own != REACH:
            edge = lax.dynamic_slice_in_dim(cells, jnp.where(side > 0, own - REACH, 0), REACH, dim)
        got.append(lax.ppermute(edge, AXES, swaps(axis, parity)))
    return got


def split(value):
    high = value.astype(jnp.bfloat16)
    return high, (value - high.astype(jnp.float32)).astype(jnp.bfloat16)


def dot(left, right):
    return lax.dot_general(left, right, (((1,), (0,)), ((), ())), preferred_element_type=jnp.float32)


def prepare_kernel(grad_ref, right_ref, left_ref):
    atoms, entries, orb, _ = grad_ref.shape
    for a in range(atoms):
        for k in range(entries):
            high, low = split(grad_ref[a, k])
            left_ref[a, :orb, k * orb : (k + 1) * orb] = high
            left_ref[a, orb:, k * orb : (k + 1) * orb] = low
            high, low = split(grad_ref[a, k].T)
            right_ref[a, k, :, :orb] = high
            right_ref[a, k, :, orb:] = low


def prepare(grad_h):
    atoms, entries, orb, _ = grad_h.shape
    return pl.pallas_call(
        prepare_kernel,
        out_shape=(
            at_hand((atoms, entries, orb, 2 * orb), jnp.bfloat16),
            at_hand((atoms, 2 * orb, entries * orb), jnp.bfloat16),
        ),
        in_specs=[VMEM],
        out_specs=(VMEM, VMEM),
        compiler_params=PARAMS,
        name="prepare",
    )(grad_h)


def sandwich_kernel(index_ref, right_ref, left_ref, own_ref, one_ref, two_ref, out_ref, green_ref, rest_ref, high_ref, low_ref):
    energies, atoms, orb, _ = out_ref.shape
    entries = right_ref.shape[1]
    places = index_ref[...]
    at = 0
    for ref in (own_ref, one_ref, two_ref):
        for a in range(ref.shape[1]):
            for e in range(energies):
                high, low = split(ref[e, a])
                green_ref[at, e * orb : (e + 1) * orb] = high
                rest_ref[at, e * orb : (e + 1) * orb] = low
            at += 1
    for a in range(atoms):
        for k in range(entries):
            weight = right_ref[a, k]
            n = places[a, k]
            both = dot(jnp.concatenate([green_ref[n], rest_ref[n]], axis=1), jnp.concatenate([weight, weight], axis=0))
            high, low = split(both[:, :orb] + both[:, orb:])
            for e in range(energies):
                high_ref[a, e, k * orb : (k + 1) * orb] = high[e * orb : (e + 1) * orb]
                low_ref[a, e, k * orb : (k + 1) * orb] = low[e * orb : (e + 1) * orb]
    for a in range(atoms):
        main = dot(left_ref[a], jnp.concatenate([high_ref[a, e] for e in range(energies)], axis=1))
        total = main[:orb] + (main[orb:] + dot(left_ref[a, :orb], jnp.concatenate([low_ref[a, e] for e in range(energies)], axis=1)))
        for e in range(energies):
            out_ref[e, a] = total[:, e * orb : (e + 1) * orb]


def sandwich(index, right, left, own, one, two):
    energies, atoms, orb, _ = own.shape
    entries = right.shape[1]
    sources = atoms + one.shape[1] + two.shape[1]
    return pl.pallas_call(
        sandwich_kernel,
        out_shape=at_hand(own.shape),
        in_specs=[VMEM] * 6,
        out_specs=VMEM,
        scratch_shapes=[
            pltpu.VMEM((sources, energies * orb, orb), jnp.bfloat16),
            pltpu.VMEM((sources, energies * orb, orb), jnp.bfloat16),
            pltpu.VMEM((atoms, energies, entries * orb, orb), jnp.bfloat16),
            pltpu.VMEM((atoms, energies, entries * orb, orb), jnp.bfloat16),
        ],
        compiler_params=PARAMS,
        name="sandwich",
    )(*near(index, right, left, own, one, two))


def parts_kernel(green_ref, real_ref, imag_ref, sems):
    copies = [pltpu.make_async_copy(green_ref.at[:, :, c], ref, sems.at[c]) for c, ref in enumerate((real_ref, imag_ref))]
    for copy in copies:
        copy.start()
    for copy in copies:
        copy.wait()


def parts(green):
    shape = green.shape[:2] + green.shape[3:]
    return pl.pallas_call(
        parts_kernel,
        out_shape=(at_hand(shape), at_hand(shape)),
        in_specs=[pl.BlockSpec(memory_space=pltpu.HBM)],
        out_specs=(VMEM, VMEM),
        scratch_shapes=[pltpu.SemaphoreType.DMA((2,))],
        compiler_params=PARAMS,
        name="parts",
    )(pltpu.with_memory_space_constraint(green, pltpu.HBM))


def shifted(weight_ref, refs, e, a):
    sources = [(ref, s) for ref in refs for s in range(ref.shape[0])]
    total = weight_ref[e : e + 1, :1] * sources[0][0][sources[0][1], a]
    for at, (ref, s) in enumerate(sources[1:]):
        total = total + weight_ref[e : e + 1, at + 1 : at + 2] * ref[s, a]
    return total


def shift_sum_kernel(weight_ref, own_ref, one_ref, two_ref, out_ref):
    for e in range(out_ref.shape[0]):
        for a in range(out_ref.shape[1]):
            out_ref[e, a] = shifted(weight_ref, (own_ref, one_ref, two_ref), e, a)


def shift_sum(weights, own, one, two):
    return pl.pallas_call(
        shift_sum_kernel,
        out_shape=at_hand(own.shape),
        in_specs=[VMEM] * 4,
        out_specs=VMEM,
        compiler_params=PARAMS,
        name="shift_sum",
    )(*near(weights, own, one, two))


def complex_product(left, right):
    high, low = split(jnp.concatenate(left, axis=1))
    block = jnp.concatenate([jnp.concatenate(right, axis=1), jnp.concatenate([-right[1], right[0]], axis=1)], axis=0)
    block_high, block_low = split(block)
    orb = left[0].shape[0]
    main = dot(jnp.concatenate([high, low], axis=0), block_high)
    total = main[:orb] + (main[orb:] + dot(high, block_low))
    return total[:, :orb], total[:, orb:]


def dyson_kernel(weight_ref, sigma_ref, own_ref, one_ref, two_ref, real_ref, imag_ref, *out_refs):
    for e in range(real_ref.shape[0]):
        for a in range(real_ref.shape[1]):
            sigma = (sigma_ref[e, a], shifted(weight_ref, (own_ref, one_ref, two_ref), e, a))
            base = (real_ref[e, a], imag_ref[e, a])
            moved = complex_product(complex_product(base, sigma), base)
            for c in range(2):
                if len(out_refs) == 2:
                    out_refs[c][e, a] = base[c] + moved[c]
                else:
                    out_refs[0][e, a, c] = base[c] + moved[c]


def dyson(weights, sigma, own, one, two, base, whole):
    shape = base[0].shape
    if whole:
        out_shape = jax.ShapeDtypeStruct(shape[:2] + (2,) + shape[2:], jnp.float32)
    else:
        out_shape = (at_hand(shape), at_hand(shape))
    return pl.pallas_call(
        dyson_kernel,
        out_shape=out_shape,
        in_specs=[VMEM] * 7,
        out_specs=VMEM if whole else (VMEM, VMEM),
        compiler_params=PARAMS,
        name="dyson",
    )(*near(weights, sigma, own, one, two, *base))


def source_index(neighbours, atoms):
    away = neighbours - lax.axis_index("space") * atoms
    first, _ = partners("space")
    below = jnp.where(first < 0, atoms, atoms + REACH) + away + REACH
    above = jnp.where(first > 0, atoms, atoms + REACH) + away - atoms
    return jnp.where(away < 0, below, jnp.where(away < atoms, away, above)).astype(jnp.int32)


def shift_weights(shifts, coupling, energies):
    here, last = lax.axis_index("energy"), lax.axis_size("energy") - 1
    columns = [(jnp.arange(energies), True)]
    for side in partners("energy"):
        start = jnp.where(side > 0, energies, -REACH)
        there = here + side
        columns.append((start + jnp.arange(REACH), (there >= 0) & (there <= last)))
    source = jnp.concatenate([c for c, _ in columns])
    valid = jnp.concatenate([jnp.broadcast_to(jnp.asarray(v), c.shape) for c, v in columns])
    distance = source[None, :] - jnp.arange(energies)[:, None]
    hit = (distance[:, :, None] == shifts) & valid[None, :, None]
    return jnp.sum(jnp.where(hit, coupling, 0.0), axis=-1)


def per_device(green0, grad_h, neighbours, shifts, coupling):
    energies, atoms = green0.shape[:2]
    base = real, imag = parts(green0)
    right, left = prepare(grad_h)
    index = source_index(neighbours, atoms)
    weights = shift_weights(shifts, coupling, energies)
    for step in range(ITERS):
        real_beside = trade(real, "energy", 0)
        imag_beside = trade(imag, "space", 1)
        summed = shift_sum(weights, real, *real_beside)
        summed_beside = trade(summed, "space", 1)
        inner = sandwich(index, right, left, imag, *imag_beside)
        inner_beside = trade(inner, "energy", 0)
        sigma = sandwich(index, right, left, summed, *summed_beside)
        green = dyson(weights, sigma, inner, *inner_beside, base, step == ITERS - 1)
        if step < ITERS - 1:
            real, imag = green
    return green


def solution(mesh):
    return jax.shard_map(
        per_device,
        mesh=mesh,
        in_specs=(
            P("energy", "space", None, None, None),
            P("space", None, None, None),
            P("space", None),
            P(),
            P(),
        ),
        out_specs=P("energy", "space", None, None, None),
        check_vma=False,
    )
```

```python
import jax
import jax.numpy as jnp
from jax import lax
from jax.experimental import pallas as pl
from jax.experimental.pallas import tpu as pltpu
from jax.sharding import PartitionSpec as P

AXES = ("energy", "space")
REACH = 2
ITERS = 2
VMEM = pl.BlockSpec(memory_space=pltpu.VMEM)
SMEM = pl.BlockSpec(memory_space=pltpu.SMEM)
PARAMS = pltpu.CompilerParams(vmem_limit_bytes=24 << 20)


def near(*arrays):
    return [pltpu.with_memory_space_constraint(a, pltpu.VMEM) for a in arrays]


def at_hand(shape, dtype=jnp.float32):
    return pltpu.VMEM(shape, dtype)


def swaps(axis, parity):
    sizes = {name: lax.axis_size(name) for name in AXES}
    count, pairs = sizes[axis], []
    for energy in range(sizes["energy"]):
        for space in range(sizes["space"]):
            to = {"energy": energy, "space": space}
            there = to[axis] + (1 if to[axis] % 2 == parity else -1)
            if 0 <= there < count:
                to[axis] = there
            elif axis == "space" and sizes["energy"] % 2 == 0:
                to["energy"] = energy ^ 1
            elif axis == "energy" and count % 2 == 0:
                to["space"] = space ^ 1
            pairs.append((energy * sizes["space"] + space, to["energy"] * sizes["space"] + to["space"]))
    return pairs


def partners(axis):
    even = lax.axis_index(axis) % 2 == 0
    first = jnp.where(even, 1, -1)
    return first, -first


def trade(cells, axis, dim):
    own, got = cells.shape[dim], []
    for parity, side in enumerate(partners(axis)):
        edge = cells
        if own != REACH:
            edge = lax.dynamic_slice_in_dim(cells, jnp.where(side > 0, own - REACH, 0), REACH, dim)
        got.append(lax.ppermute(edge, AXES, swaps(axis, parity)))
    return got


def split(value):
    high = value.astype(jnp.bfloat16)
    return high, (value - high.astype(jnp.float32)).astype(jnp.bfloat16)


def dot(left, right):
    return lax.dot_general(left, right, (((1,), (0,)), ((), ())), preferred_element_type=jnp.float32)


def prepare_kernel(grad_ref, right_ref, left_ref):
    atoms, entries, orb, _ = grad_ref.shape
    for a in range(atoms):
        for k in range(entries):
            high, low = split(grad_ref[a, k])
            left_ref[a, :orb, k * orb : (k + 1) * orb] = high
            left_ref[a, orb:, k * orb : (k + 1) * orb] = low
            high, low = split(grad_ref[a, k].T)
            right_ref[a, k, :, :orb] = high
            right_ref[a, k, :, orb:] = low


def prepare(grad_h):
    atoms, entries, orb, _ = grad_h.shape
    return pl.pallas_call(
        prepare_kernel,
        out_shape=(
            at_hand((atoms, entries, orb, 2 * orb), jnp.bfloat16),
            at_hand((atoms, 2 * orb, entries * orb), jnp.bfloat16),
        ),
        in_specs=[VMEM],
        out_specs=(VMEM, VMEM),
        compiler_params=PARAMS,
        name="prepare",
    )(grad_h)


def sandwich_kernel(index_ref, right_ref, left_ref, *refs):
    *in_refs, out_ref, green_ref, rest_ref, high_ref, low_ref = refs
    energies, atoms, orb, _ = out_ref.shape
    entries = right_ref.shape[1]
    places = index_ref[...]
    sources = [(ref, i) for ref in in_refs for i in range(ref.shape[1])]
    for at, (ref, i) in enumerate(sources):
        for e in range(energies):
            high, low = split(ref[e, i])
            green_ref[at, e * orb : (e + 1) * orb] = high
            rest_ref[at, e * orb : (e + 1) * orb] = low
    for a in range(atoms):
        for k in range(entries):
            weight = right_ref[a, k]
            n = places[a, k]
            both = dot(jnp.concatenate([green_ref[n], rest_ref[n]], axis=1), jnp.concatenate([weight, weight], axis=0))
            high, low = split(both[:, :orb] + both[:, orb:])
            for e in range(energies):
                high_ref[a, e, k * orb : (k + 1) * orb] = high[e * orb : (e + 1) * orb]
                low_ref[a, e, k * orb : (k + 1) * orb] = low[e * orb : (e + 1) * orb]
    for a in range(atoms):
        highs, lows = (jnp.concatenate([ref[a, e] for e in range(energies)], axis=1) for ref in (high_ref, low_ref))
        main = dot(left_ref[a], highs)
        total = main[:orb] + (main[orb:] + dot(left_ref[a, :orb], lows))
        for e in range(energies):
            out_ref[e, a] = total[:, e * orb : (e + 1) * orb]


def sandwich(index, right, left, own, one, two):
    energies, atoms, orb, _ = own.shape
    entries = right.shape[1]
    count = atoms + one.shape[1] + two.shape[1]
    return pl.pallas_call(
        sandwich_kernel,
        out_shape=at_hand(own.shape),
        in_specs=[VMEM] * 6,
        out_specs=VMEM,
        scratch_shapes=[
            pltpu.VMEM((count, energies * orb, orb), jnp.bfloat16),
            pltpu.VMEM((count, energies * orb, orb), jnp.bfloat16),
            pltpu.VMEM((atoms, energies, entries * orb, orb), jnp.bfloat16),
            pltpu.VMEM((atoms, energies, entries * orb, orb), jnp.bfloat16),
        ],
        compiler_params=PARAMS,
        name="sandwich",
    )(*near(index, right, left, own, one, two))


def parts_kernel(green_ref, real_ref, imag_ref, sems):
    copies = [pltpu.make_async_copy(green_ref.at[:, :, c], ref, sems.at[c]) for c, ref in enumerate((real_ref, imag_ref))]
    for copy in copies:
        copy.start()
    for copy in copies:
        copy.wait()


def parts(green):
    shape = green.shape[:2] + green.shape[3:]
    return pl.pallas_call(
        parts_kernel,
        out_shape=(at_hand(shape), at_hand(shape)),
        in_specs=[pl.BlockSpec(memory_space=pltpu.HBM)],
        out_specs=(VMEM, VMEM),
        scratch_shapes=[pltpu.SemaphoreType.DMA((2,))],
        compiler_params=PARAMS,
        name="parts",
    )(pltpu.with_memory_space_constraint(green, pltpu.HBM))


def weighted(weight_ref, e, blocks):
    total = weight_ref[e : e + 1, :1] * blocks[0]
    for at, block in enumerate(blocks[1:]):
        total = total + weight_ref[e : e + 1, at + 1 : at + 2] * block
    return total


def sources_of(refs, a):
    return [ref[s, a] for ref in refs for s in range(ref.shape[0])]


def shift_sum_kernel(weight_ref, own_ref, one_ref, two_ref, out_ref):
    for e in range(out_ref.shape[0]):
        for a in range(out_ref.shape[1]):
            out_ref[e, a] = weighted(weight_ref, e, sources_of((own_ref, one_ref, two_ref), a))


def shift_sum(weights, own, one, two):
    return pl.pallas_call(
        shift_sum_kernel,
        out_shape=at_hand(own.shape),
        in_specs=[VMEM] * 4,
        out_specs=VMEM,
        compiler_params=PARAMS,
        name="shift_sum",
    )(*near(weights, own, one, two))


def complex_product(left, right):
    high, low = split(jnp.concatenate(left, axis=1))
    block = jnp.concatenate([jnp.concatenate(right, axis=1), jnp.concatenate([-right[1], right[0]], axis=1)], axis=0)
    block_high, block_low = split(block)
    orb = left[0].shape[0]
    main = dot(jnp.concatenate([high, low], axis=0), block_high)
    total = main[:orb] + (main[orb:] + dot(high, block_low))
    return total[:, :orb], total[:, orb:]


def dyson_kernel(weight_ref, sigma_ref, own_ref, one_ref, two_ref, real_ref, imag_ref, *out_refs):
    energies, atoms = real_ref.shape[:2]
    cells = [(e, a) for e in range(energies) for a in range(atoms)]
    base = {at: (real_ref[at], imag_ref[at]) for at in cells}
    moved = {}
    for e, a in cells:
        sigma = (sigma_ref[e, a], weighted(weight_ref, e, sources_of((own_ref, one_ref, two_ref), a)))
        moved[e, a] = complex_product(base[e, a], sigma)
    copies = []
    for at in cells:
        real, imag = (old + new for old, new in zip(base[at], complex_product(moved[at], base[at])))
        if len(out_refs) == 2:
            out_refs[0][at], out_refs[1][at] = real, imag
        else:
            out_ref, stage_ref, sems = out_refs
            stage_ref[*at, 0], stage_ref[*at, 1] = real, imag
            copies.append(pltpu.make_async_copy(stage_ref.at[*at], out_ref.at[*at], sems.at[len(copies)]))
            copies[-1].start()
    for copy in copies:
        copy.wait()


def dyson(weights, sigma, own, one, two, base, whole):
    energies, atoms, orb, _ = sigma.shape
    out_shape, out_specs, scratch = (at_hand(sigma.shape), at_hand(sigma.shape)), (VMEM, VMEM), []
    if whole:
        out_shape = jax.ShapeDtypeStruct((energies, atoms, 2, orb, orb), jnp.float32)
        out_specs = pl.BlockSpec(memory_space=pltpu.HBM)
        scratch = [pltpu.VMEM(out_shape.shape, jnp.float32), pltpu.SemaphoreType.DMA((energies * atoms,))]
    return pl.pallas_call(
        dyson_kernel,
        out_shape=out_shape,
        in_specs=[VMEM] * 7,
        out_specs=out_specs,
        scratch_shapes=scratch,
        compiler_params=PARAMS,
        name="dyson",
    )(*near(weights, sigma, own, one, two, *base))


def source_index(neighbours, atoms):
    away = neighbours - lax.axis_index("space") * atoms
    first, _ = partners("space")
    below = jnp.where(first < 0, atoms, atoms + REACH) + away + REACH
    above = jnp.where(first > 0, atoms, atoms + REACH) + away - atoms
    return jnp.where(away < 0, below, jnp.where(away < atoms, away, above)).astype(jnp.int32)


def shift_weights(shifts, coupling, energies):
    here, last = lax.axis_index("energy"), lax.axis_size("energy") - 1
    columns = [(jnp.arange(energies), True)]
    for side in partners("energy"):
        start = jnp.where(side > 0, energies, -REACH)
        there = here + side
        columns.append((start + jnp.arange(REACH), (there >= 0) & (there <= last)))
    source = jnp.concatenate([c for c, _ in columns])
    valid = jnp.concatenate([jnp.broadcast_to(jnp.asarray(v), c.shape) for c, v in columns])
    distance = source[None, :] - jnp.arange(energies)[:, None]
    hit = (distance[:, :, None] == shifts) & valid[None, :, None]
    return jnp.sum(jnp.where(hit, coupling, 0.0), axis=-1)


def per_device(green0, grad_h, neighbours, shifts, coupling):
    energies, atoms = green0.shape[:2]
    base = real, imag = parts(green0)
    right, left = prepare(grad_h)
    index = source_index(neighbours, atoms)
    weights = shift_weights(shifts, coupling, energies)
    for step in range(ITERS):
        real_beside = trade(real, "energy", 0)
        imag_beside = trade(imag, "space", 1)
        summed = shift_sum(weights, real, *real_beside)
        summed_beside = trade(summed, "space", 1)
        inner = sandwich(index, right, left, imag, *imag_beside)
        inner_beside = trade(inner, "energy", 0)
        sigma = sandwich(index, right, left, summed, *summed_beside)
        green = dyson(weights, sigma, inner, *inner_beside, base, step == ITERS - 1)
        if step < ITERS - 1:
            real, imag = green
    return green


def solution(mesh):
    return jax.shard_map(
        per_device,
        mesh=mesh,
        in_specs=(
            P("energy", "space", None, None, None),
            P("space", None, None, None),
            P("space", None),
            P(),
            P(),
        ),
        out_specs=P("energy", "space", None, None, None),
        check_vma=False,
    )
```

```python
import jax
import jax.numpy as jnp
from jax import lax
from jax.experimental import pallas as pl
from jax.experimental.pallas import tpu as pltpu
from jax.sharding import PartitionSpec as P

AXES = ("energy", "space")
REACH = 2
ITERS = 2
VMEM = pl.BlockSpec(memory_space=pltpu.VMEM)
SMEM = pl.BlockSpec(memory_space=pltpu.SMEM)
PARAMS = pltpu.CompilerParams(vmem_limit_bytes=24 << 20)


def near(*arrays):
    return [pltpu.with_memory_space_constraint(a, pltpu.VMEM) for a in arrays]


def at_hand(shape, dtype=jnp.float32):
    return pltpu.VMEM(shape, dtype)


def swaps(axis, parity):
    sizes = {name: lax.axis_size(name) for name in AXES}
    count, pairs = sizes[axis], []
    for energy in range(sizes["energy"]):
        for space in range(sizes["space"]):
            to = {"energy": energy, "space": space}
            there = to[axis] + (1 if to[axis] % 2 == parity else -1)
            if 0 <= there < count:
                to[axis] = there
            elif axis == "space" and sizes["energy"] % 2 == 0:
                to["energy"] = energy ^ 1
            elif axis == "energy" and sizes["space"] % 2 == 0:
                to["space"] = space ^ 1
            pairs.append((energy * sizes["space"] + space, to["energy"] * sizes["space"] + to["space"]))
    return pairs


def partners(axis):
    even = lax.axis_index(axis) % 2 == 0
    first = jnp.where(even, 1, -1)
    return first, -first


def trade(cells, axis, dim):
    own, got = cells.shape[dim], []
    for parity, side in enumerate(partners(axis)):
        edge = cells
        if own != REACH:
            edge = lax.dynamic_slice_in_dim(cells, jnp.where(side > 0, own - REACH, 0), REACH, dim)
        got.append(lax.ppermute(edge, AXES, swaps(axis, parity)))
    return got


def split(value):
    high = value.astype(jnp.bfloat16)
    return high, (value - high.astype(jnp.float32)).astype(jnp.bfloat16)


def dot(left, right):
    return lax.dot_general(left, right, (((1,), (0,)), ((), ())), preferred_element_type=jnp.float32)


def prepare_kernel(grad_ref, right_ref, left_ref):
    atoms, entries, orb, _ = grad_ref.shape
    for a in range(atoms):
        for k in range(entries):
            high, low = split(grad_ref[a, k])
            left_ref[a, k, :orb] = high
            left_ref[a, k, orb:] = low
            high, low = split(grad_ref[a, k].T)
            right_ref[a, k, 0] = high
            right_ref[a, k, 1] = low


def prepare(grad_h):
    atoms, entries, orb, _ = grad_h.shape
    return pl.pallas_call(
        prepare_kernel,
        out_shape=(
            at_hand((atoms, entries, 2, orb, orb), jnp.bfloat16),
            at_hand((atoms, entries, 2 * orb, orb), jnp.bfloat16),
        ),
        in_specs=[VMEM],
        out_specs=(VMEM, VMEM),
        compiler_params=PARAMS,
        name="prepare",
    )(grad_h)


def sandwich_kernel(index_ref, right_ref, left_ref, *refs):
    *in_refs, out_ref, green_ref, rest_ref, high_ref, low_ref = refs
    energies, atoms, orb, _ = out_ref.shape
    entries = right_ref.shape[1]
    places = index_ref[...]
    sources = [(ref, i) for ref in in_refs for i in range(ref.shape[1])]
    for at, (ref, i) in enumerate(sources):
        for e in range(energies):
            high, low = split(ref[e, i])
            green_ref[at, e * orb : (e + 1) * orb] = high
            rest_ref[at, e * orb : (e + 1) * orb] = low
    for a in range(atoms):
        for k in range(entries):
            weight = jnp.concatenate([right_ref[a, k, 0], right_ref[a, k, 1]], axis=1)
            n = places[a, k]
            both = dot(jnp.concatenate([green_ref[n], rest_ref[n]], axis=1), jnp.concatenate([weight, weight], axis=0))
            high, low = split(both[:, :orb] + both[:, orb:])
            for e in range(energies):
                high_ref[a, e, k * orb : (k + 1) * orb] = high[e * orb : (e + 1) * orb]
                low_ref[a, e, k * orb : (k + 1) * orb] = low[e * orb : (e + 1) * orb]
    for a in range(atoms):
        highs, lows = (jnp.concatenate([ref[a, e] for e in range(energies)], axis=1) for ref in (high_ref, low_ref))
        left = jnp.concatenate([left_ref[a, k] for k in range(entries)], axis=1)
        main = dot(left, highs)
        total = main[:orb] + (main[orb:] + dot(left[:orb], lows))
        for e in range(energies):
            out_ref[e, a] = total[:, e * orb : (e + 1) * orb]


def sandwich(index, right, left, own, one, two):
    energies, atoms, orb, _ = own.shape
    entries = right.shape[1]
    count = atoms + one.shape[1] + two.shape[1]
    return pl.pallas_call(
        sandwich_kernel,
        out_shape=at_hand(own.shape),
        in_specs=[VMEM] * 6,
        out_specs=VMEM,
        scratch_shapes=[
            pltpu.VMEM((count, energies * orb, orb), jnp.bfloat16),
            pltpu.VMEM((count, energies * orb, orb), jnp.bfloat16),
            pltpu.VMEM((atoms, energies, entries * orb, orb), jnp.bfloat16),
            pltpu.VMEM((atoms, energies, entries * orb, orb), jnp.bfloat16),
        ],
        compiler_params=PARAMS,
        name="sandwich",
    )(*near(index, right, left, own, one, two))


def parts_kernel(green_ref, real_ref, imag_ref, sems):
    copies = [pltpu.make_async_copy(green_ref.at[:, :, c], ref, sems.at[c]) for c, ref in enumerate((real_ref, imag_ref))]
    for copy in copies:
        copy.start()
    for copy in copies:
        copy.wait()


def parts(green):
    shape = green.shape[:2] + green.shape[3:]
    return pl.pallas_call(
        parts_kernel,
        out_shape=(at_hand(shape), at_hand(shape)),
        in_specs=[pl.BlockSpec(memory_space=pltpu.HBM)],
        out_specs=(VMEM, VMEM),
        scratch_shapes=[pltpu.SemaphoreType.DMA((2,))],
        compiler_params=PARAMS,
        name="parts",
    )(pltpu.with_memory_space_constraint(green, pltpu.HBM))


def weighted(weight_ref, e, blocks):
    total = weight_ref[e : e + 1, :1] * blocks[0]
    for at, block in enumerate(blocks[1:]):
        total = total + weight_ref[e : e + 1, at + 1 : at + 2] * block
    return total


def sources_of(refs, a):
    return [ref[s, a] for ref in refs for s in range(ref.shape[0])]


def shift_sum_kernel(weight_ref, own_ref, one_ref, two_ref, out_ref):
    for e in range(out_ref.shape[0]):
        for a in range(out_ref.shape[1]):
            out_ref[e, a] = weighted(weight_ref, e, sources_of((own_ref, one_ref, two_ref), a))


def shift_sum(weights, own, one, two):
    return pl.pallas_call(
        shift_sum_kernel,
        out_shape=at_hand(own.shape),
        in_specs=[VMEM] * 4,
        out_specs=VMEM,
        compiler_params=PARAMS,
        name="shift_sum",
    )(*near(weights, own, one, two))


def complex_product(left, right):
    high, low = split(jnp.concatenate(left, axis=1))
    block = jnp.concatenate([jnp.concatenate(right, axis=1), jnp.concatenate([-right[1], right[0]], axis=1)], axis=0)
    block_high, block_low = split(block)
    orb = left[0].shape[0]
    main = dot(jnp.concatenate([high, low], axis=0), block_high)
    total = main[:orb] + (main[orb:] + dot(high, block_low))
    return total[:, :orb], total[:, orb:]


def dyson_kernel(weight_ref, sigma_ref, own_ref, one_ref, two_ref, real_ref, imag_ref, *out_refs):
    energies, atoms = real_ref.shape[:2]
    cells = [(e, a) for e in range(energies) for a in range(atoms)]
    base = {at: (real_ref[at], imag_ref[at]) for at in cells}
    moved = {}
    for e, a in cells:
        sigma = (sigma_ref[e, a], weighted(weight_ref, e, sources_of((own_ref, one_ref, two_ref), a)))
        moved[e, a] = complex_product(base[e, a], sigma)
    copies = []
    for at in cells:
        real, imag = (old + new for old, new in zip(base[at], complex_product(moved[at], base[at])))
        if len(out_refs) == 2:
            out_refs[0][at], out_refs[1][at] = real, imag
        else:
            out_ref, stage_ref, sems = out_refs
            stage_ref[*at, 0], stage_ref[*at, 1] = real, imag
            copies.append(pltpu.make_async_copy(stage_ref.at[*at], out_ref.at[*at], sems.at[len(copies)]))
            copies[-1].start()
    for copy in copies:
        copy.wait()


def dyson(weights, sigma, own, one, two, base, whole):
    energies, atoms, orb, _ = sigma.shape
    out_shape, out_specs, scratch = (at_hand(sigma.shape), at_hand(sigma.shape)), (VMEM, VMEM), []
    if whole:
        out_shape = jax.ShapeDtypeStruct((energies, atoms, 2, orb, orb), jnp.float32)
        out_specs = pl.BlockSpec(memory_space=pltpu.HBM)
        scratch = [pltpu.VMEM(out_shape.shape, jnp.float32), pltpu.SemaphoreType.DMA((energies * atoms,))]
    return pl.pallas_call(
        dyson_kernel,
        out_shape=out_shape,
        in_specs=[VMEM] * 7,
        out_specs=out_specs,
        scratch_shapes=scratch,
        compiler_params=PARAMS,
        name="dyson",
    )(*near(weights, sigma, own, one, two, *base))


def source_index(neighbours, atoms):
    away = neighbours - lax.axis_index("space") * atoms
    first, _ = partners("space")
    below = jnp.where(first < 0, atoms, atoms + REACH) + away + REACH
    above = jnp.where(first > 0, atoms, atoms + REACH) + away - atoms
    return jnp.where(away < 0, below, jnp.where(away < atoms, away, above)).astype(jnp.int32)


def shift_weights(shifts, coupling, energies):
    here, last = lax.axis_index("energy"), lax.axis_size("energy") - 1
    columns = [(jnp.arange(energies), True)]
    for side in partners("energy"):
        start = jnp.where(side > 0, energies, -REACH)
        there = here + side
        columns.append((start + jnp.arange(REACH), (there >= 0) & (there <= last)))
    source = jnp.concatenate([c for c, _ in columns])
    valid = jnp.concatenate([jnp.broadcast_to(jnp.asarray(v), c.shape) for c, v in columns])
    distance = source[None, :] - jnp.arange(energies)[:, None]
    hit = (distance[:, :, None] == shifts) & valid[None, :, None]
    return jnp.sum(jnp.where(hit, coupling, 0.0), axis=-1)


def per_device(green0, grad_h, neighbours, shifts, coupling):
    energies, atoms = green0.shape[:2]
    base = real, imag = parts(green0)
    right, left = prepare(grad_h)
    index = source_index(neighbours, atoms)
    weights = shift_weights(shifts, coupling, energies)
    for step in range(ITERS):
        real_beside = trade(real, "energy", 0)
        imag_beside = trade(imag, "space", 1)
        summed = shift_sum(weights, real, *real_beside)
        summed_beside = trade(summed, "space", 1)
        inner = sandwich(index, right, left, imag, *imag_beside)
        inner_beside = trade(inner, "energy", 0)
        sigma = sandwich(index, right, left, summed, *summed_beside)
        green = dyson(weights, sigma, inner, *inner_beside, base, step == ITERS - 1)
        if step < ITERS - 1:
            real, imag = green
    return green


def solution(mesh):
    return jax.shard_map(
        per_device,
        mesh=mesh,
        in_specs=(
            P("energy", "space", None, None, None),
            P("space", None, None, None),
            P("space", None),
            P(),
            P(),
        ),
        out_specs=P("energy", "space", None, None, None),
        check_vma=False,
    )
```
